32 devices in a mesh: chan: 8 (over z, core), ctx: 4 (over y, x).
Axes of the slice: x: 2, y: 2, z: 4, core: 2. Of those that a mesh axis runs over, the one named last changes fastest.
Arguments:
- saved_input: float32 [2, 128, 32768], P(None, 'chan', 'ctx'), may hold values from -6 to 6
- out_grad: float32 [2, 128, 32768], P(None, 'chan', 'ctx'), may hold values from -6 to 6
- filters: float32 [2, 32768], P(None, 'ctx'), may hold values from -0.03125 to 0.03125
Outputs:
- input_grad: bfloat16 [2, 128, 32768], P(None, 'chan', 'ctx')
- filter_grad: float32 [2, 32768], P(None, 'ctx')
The draws below stay inside these ranges and needn't reach their ends.
All inputs are finite; a program needn't handle non-finite values.
Results may differ from the reference program's by a relative error of at most 0.001.
Values sent between devices are 32-bit elements; how exact they have to be, the bound alone decides.
A program may use at most 128 MiB of HBM per device.

```python
import jax
import jax.numpy as jnp
from jax import lax

BATCH = 2
GROUPS = 2
CHANNELS = 128
LENGTH = 32768


def level_of(rng, dims, cuts, low, top_value):
    def one(position, parts):
        heights = jax.random.uniform(jax.random.fold_in(jax.random.fold_in(rng, 6), position), (parts,), jnp.float32, low / len(cuts), top_value / len(cuts))
        return jnp.repeat(jnp.exp(heights), dims[position] // parts).reshape((-1,) + (1,) * (len(dims) - position - 1))

    loudness = one(*cuts[0])
    for cut in cuts[1:]:
        loudness = loudness * one(*cut)
    return loudness


def scatter_about(stream_key, extent, scale, bound, pieces=(), held_as=jnp.bfloat16):
    factor_of = level_of(stream_key, extent, pieces, -0.22, 0.18) if pieces else 1.0
    array = jax.random.normal(stream_key, extent, jnp.float32) * scale * factor_of
    return jnp.minimum(jnp.maximum(array, -bound), bound).astype(held_as)


def setup_inputs(seed: int = 0) -> dict:
    arg_keys = jax.random.split(jax.random.key(seed), 4)
    return {
        "saved_input": scatter_about(arg_keys[0], (BATCH, CHANNELS, LENGTH), 1.0, 6.0, ((1, 8), (2, 4)), jnp.float32),
        "out_grad": scatter_about(arg_keys[1], (BATCH, CHANNELS, LENGTH), 1.0, 6.0, ((1, 8), (2, 4)), jnp.float32),
        "filters": scatter_about(arg_keys[2], (GROUPS, LENGTH), LENGTH ** -0.5, 0.03125, ((1, 4),), jnp.float32),
    }


def reference(saved_input, out_grad, filters):
    points = 2 * LENGTH
    per_filter = CHANNELS // GROUPS
    filter_spec = jnp.fft.rfft(filters.astype(jnp.float32), n=points, axis=-1)
    inputs = saved_input.astype(jnp.float32).reshape(BATCH, per_filter, GROUPS, LENGTH).transpose(1, 0, 2, 3)
    gradients = out_grad.astype(jnp.float32).reshape(BATCH, per_filter, GROUPS, LENGTH).transpose(1, 0, 2, 3)

    def one_block(running, block_pair):
        block_in, block_grad = block_pair
        in_spec = jnp.fft.rfft(block_in, n=points, axis=-1)
        grad_spec = jnp.fft.rfft(block_grad, n=points, axis=-1)
        input_part = jnp.fft.irfft(jnp.conj(filter_spec)[None] * grad_spec, n=points, axis=-1)[..., :LENGTH]
        filter_part = jnp.fft.irfft(jnp.sum(jnp.conj(in_spec) * grad_spec, axis=0), n=points, axis=-1)[..., :LENGTH]
        return running + filter_part, input_part.astype(jnp.bfloat16)

    filter_total, input_blocks = lax.scan(one_block, jnp.zeros((GROUPS, LENGTH), jnp.float32), (inputs, gradients))
    input_grad = input_blocks.transpose(1, 0, 2, 3).reshape(BATCH, CHANNELS, LENGTH)
    norm_factor = float(LENGTH * BATCH * per_filter) ** -0.5
    return input_grad, filter_total * norm_factor
```

```python
import functools
import math

import jax
import jax.numpy as jnp
import numpy as np
from jax import lax
from jax.experimental import pallas as pl
from jax.experimental.pallas import tpu as pltpu
from jax.sharding import PartitionSpec as P

LANES = 256
TILE = 128
F32 = jnp.float32
BF16 = jnp.bfloat16


def split_table(table):
    high = table.astype(np.float32).astype(BF16)
    low = (table - high.astype(np.float64)).astype(np.float32).astype(BF16)
    return high, low


def tables(n1, n2):
    length = n1 * n2
    a = np.arange(n1, dtype=np.int64)
    b = np.arange(n2, dtype=np.int64)
    theta = 2.0 * np.pi / (4 * n1) * (np.outer(4 * a + 1, a) % (4 * n1))
    cosine, sine = np.cos(theta), np.sin(theta)
    high, low = split_table(np.concatenate([cosine, -sine], axis=0))
    first = np.concatenate([high, high, low], axis=1)
    high, low = split_table(np.concatenate([cosine.T, sine.T], axis=1) / length)
    last = np.concatenate([high, high, low], axis=1)
    turn = 2.0 * np.pi / (4 * length) * (np.outer(4 * a + 1, b) % (4 * length))
    turn_re = np.cos(turn).astype(np.float32)
    turn_im = (-np.sin(turn)).astype(np.float32)
    phi = 2.0 * np.pi / n2 * (np.outer(b, b) % n2)
    re, im = np.cos(phi), -np.sin(phi)
    mid_high, mid_low = split_table(np.block([[re, im], [-im, re]]))
    return first, last, turn_re, turn_im, mid_high, mid_low


def split(x):
    high = x.astype(BF16)
    return high, (x - high.astype(F32)).astype(BF16)


def dot(a, b):
    return jnp.dot(a, b, preferred_element_type=F32)


def body(
    d_n, c_n, rows, n1, n2, piece, norm,
    og_hbm, sv_hbm, fl_hbm, first_ref, last_ref, tr_ref, ti_ref, mh_ref, ml_ref,
    ig_out, fg_out,
    og_buf, sv_buf, fl_buf, g_spec, h_spec, p_spec, ig_send, fp_send, fp_recv, rs_send, rs_recv, ag_send,
    loc_sem, send_sem, recv_sem, csend_sem, crecv_sem,
):
    me = lax.axis_index("ctx")
    mc = lax.axis_index("chan")
    chunk = n1 // d_n
    halves = n2 // TILE
    block = chunk * halves * rows
    both = 2 if n1 <= 128 else 1
    ahead = [lax.rem(me + o, d_n) for o in range(d_n)]
    behind = [lax.rem(me + d_n - o, d_n) for o in range(d_n)]
    cahead = [lax.rem(mc + o, c_n) for o in range(c_n)]
    cbehind = [lax.rem(mc + c_n - o, c_n) for o in range(c_n)]

    barrier = pltpu.get_barrier_semaphore()
    for o in range(1, d_n):
        pl.semaphore_signal(barrier, inc=1, device_id={"ctx": ahead[o]}, device_id_type=pl.DeviceIdType.MESH)
    for o in range(1, c_n):
        pl.semaphore_signal(barrier, inc=1, device_id={"chan": cahead[o]}, device_id_type=pl.DeviceIdType.MESH)

    def at_rows(ref, index):
        return ref.at[pl.ds(pl.multiple_of(index * block, block), block), :]

    def at_chunk(ref, index):
        return ref.at[:, pl.ds(pl.multiple_of(index * chunk, chunk), chunk), :]

    locals_ = [
        pltpu.make_async_copy(fl_hbm, at_chunk(fl_buf, me), loc_sem.at[0]),
        pltpu.make_async_copy(og_hbm.at[me], at_rows(og_buf, me), loc_sem.at[1]),
        pltpu.make_async_copy(sv_hbm.at[me], at_rows(sv_buf, me), loc_sem.at[2]),
    ]
    for copy in locals_:
        copy.start()
    pl.semaphore_wait(barrier, d_n + c_n - 2)

    def push(kind, o, src, dst):
        return pltpu.make_async_remote_copy(
            src_ref=src, dst_ref=dst, send_sem=send_sem.at[kind, o], recv_sem=recv_sem.at[kind, o],
            device_id={"ctx": ahead[o]}, device_id_type=pl.DeviceIdType.MESH)

    def cpush(kind, o, src, dst):
        return pltpu.make_async_remote_copy(
            src_ref=src, dst_ref=dst, send_sem=csend_sem.at[kind, o], recv_sem=crecv_sem.at[kind, o],
            device_id={"chan": cahead[o]}, device_id_type=pl.DeviceIdType.MESH)

    peers = range(1, d_n)
    sent = []
    for o in peers:
        sent.append(push(0, o, fl_hbm, at_chunk(fl_buf, me)))
    for o in peers:
        sent.append(push(1, o, og_hbm.at[ahead[o]], at_rows(og_buf, me)))
    for o in peers:
        sent.append(push(2, o, sv_hbm.at[ahead[o]], at_rows(sv_buf, me)))
    for copy in sent:
        copy.start()

    def first_stage(x):
        high, low = split(x)
        out = dot(first_ref[...], jnp.concatenate([high, low, high], axis=0))
        return turned(out[:n1], out[n1:])

    def turned(re, im):
        tr, ti = tr_ref[...], ti_ref[...]
        return jnp.concatenate([re * tr - im * ti, re * ti + im * tr], axis=1)

    def mid_stage(x):
        high, low = split(x)
        return dot(high, mh_ref[...]) + dot(low, mh_ref[...]) + dot(high, ml_ref[...])

    def last_stage(x):
        x = turned(x[:, :n2], x[:, n2:])
        high, low = split(jnp.concatenate([x[:, :n2], x[:, n2:]], axis=0))
        return dot(last_ref[...], jnp.concatenate([high, low, high], axis=0))

    def stacked(parts):
        return parts[0] if len(parts) == 1 else jnp.concatenate(parts, axis=0)

    def row_of(ref, r):
        parts = [ref[pl.ds(h * rows + r, n1, stride=halves * rows), :] for h in range(halves)]
        return jnp.concatenate(parts, axis=1)

    def spectra(ref, i):
        return mid_stage(stacked([first_stage(row_of(ref, i * both + j)) for j in range(both)]))

    def group_rows(i):
        return pl.ds(pl.multiple_of(lax.rem(i * both, 2) * n1, n1), both * n1)

    def span(i):
        return pl.ds(pl.multiple_of(i * (both * n1), both * n1), both * n1)

    locals_[0].wait()
    for o in peers:
        push(0, o, fl_hbm, at_chunk(fl_buf, behind[o])).wait_recv()
    for g in range(0, 2, both):
        h_spec[g * n1 : (g + both) * n1, :] = mid_stage(
            stacked([first_stage(fl_buf[g + j]) for j in range(both)]))

    locals_[1].wait()
    for o in peers:
        push(1, o, og_hbm.at[ahead[o]], at_rows(og_buf, behind[o])).wait_recv()

    def input_step(i, carry):
        grad = spectra(og_buf, i)
        g_spec[span(i), :] = grad
        filt = h_spec[group_rows(i), :]
        gr, gi, hr, hi = grad[:, :n2], grad[:, n2:], filt[:, :n2], filt[:, n2:]
        back = mid_stage(jnp.concatenate([hr * gr + hi * gi, hi * gr - hr * gi], axis=1))
        for j in range(both):
            out = last_stage(back[j * n1 : (j + 1) * n1])
            for h in range(halves):
                ig_send[pl.ds(h * rows + i * both + j, n1, stride=halves * rows), :] = out[:, h * TILE : (h + 1) * TILE]
        return carry

    lax.fori_loop(0, rows // both, input_step, 0)
    own = pltpu.make_async_copy(at_rows(ig_send, me), ig_out.at[me], loc_sem.at[3])
    own.start()
    for o in peers:
        copy = push(3, o, at_rows(ig_send, ahead[o]), ig_out.at[me])
        copy.start()
        sent.append(copy)

    locals_[2].wait()
    for o in peers:
        push(2, o, sv_hbm.at[ahead[o]], at_rows(sv_buf, behind[o])).wait_recv()
    p_spec[...] = jnp.zeros_like(p_spec)

    def filter_step(i, carry):
        spec = spectra(sv_buf, i)
        grad = g_spec[span(i), :]
        xr, xi, gr, gi = spec[:, :n2], spec[:, n2:], grad[:, :n2], grad[:, n2:]
        p_spec[group_rows(i), :] += jnp.concatenate([xr * gr + xi * gi, xi * gr - xr * gi], axis=1)
        return carry

    lax.fori_loop(0, rows // both, filter_step, 0)
    total = mid_stage(p_spec[...])
    for g in range(2):
        part = last_stage(total[g * n1 : (g + 1) * n1])
        per_chunk = chunk // piece
        for d in range(d_n):
            for p in range(per_chunk):
                start = d * chunk + p * piece
                fp_send[d, g * per_chunk + p] = part[start : start + piece, :]

    for o in peers:
        copy = push(4, o, fp_send.at[ahead[o]], fp_recv.at[me])
        copy.start()
        sent.append(copy)
    for o in peers:
        push(4, o, fp_send.at[ahead[o]], fp_recv.at[behind[o]]).wait_recv()
    acc = fp_send[me]
    for o in peers:
        acc = acc + fp_recv[behind[o]]
    rs_send[...] = acc
    for o in range(1, c_n):
        copy = cpush(0, o, rs_send.at[cahead[o]], rs_recv.at[mc])
        copy.start()
        sent.append(copy)
    for o in range(1, c_n):
        cpush(0, o, rs_send.at[cahead[o]], rs_recv.at[cbehind[o]]).wait_recv()
    acc = rs_send[mc]
    for o in range(1, c_n):
        acc = acc + rs_recv[cbehind[o]]
    acc = acc * norm
    ag_send[...] = acc
    fg_out[mc] = acc
    for o in range(1, c_n):
        copy = cpush(1, o, ag_send, fg_out.at[mc])
        copy.start()
        sent.append(copy)
    for o in range(1, c_n):
        cpush(1, o, ag_send, fg_out.at[cbehind[o]]).wait_recv()
    for o in peers:
        push(3, o, at_rows(ig_send, ahead[o]), ig_out.at[behind[o]]).wait_recv()
    own.wait()
    for copy in sent:
        copy.wait_send()


def local(saved_input, out_grad, filters):
    batch, channels, tokens = saved_input.shape
    groups = filters.shape[0]
    d_n, c_n = lax.axis_size("ctx"), lax.axis_size("chan")
    rows = batch * channels // d_n
    n2 = LANES
    chunk = tokens // n2
    n1 = chunk * d_n
    block = chunk * rows * (n2 // TILE)
    piece = groups * chunk // c_n
    assert groups == 2 and rows % 2 == 0 and channels % 2 == 0 and chunk % piece == 0
    norm = float(tokens * d_n * batch * (channels // groups) * c_n) ** -0.5

    def blocks(x):
        return x.reshape(d_n, rows, tokens // TILE, TILE).transpose(0, 2, 1, 3).reshape(d_n, block, TILE)

    first, last, turn_re, turn_im, mid_high, mid_low = tables(n1, n2)
    any_spec = pl.BlockSpec(memory_space=pl.ANY)
    vmem = pl.BlockSpec(memory_space=pltpu.VMEM)
    dma = pltpu.SemaphoreType.DMA
    input_grad, filter_grad = pl.pallas_call(
        functools.partial(body, d_n, c_n, rows, n1, n2, piece, norm),
        out_shape=[
            jax.ShapeDtypeStruct((d_n, block, TILE), F32),
            jax.ShapeDtypeStruct((c_n, piece, n2), F32),
        ],
        in_specs=[any_spec] * 3 + [vmem] * 6,
        out_specs=[any_spec, vmem],
        scratch_shapes=[
            pltpu.VMEM((d_n * block, TILE), F32),
            pltpu.VMEM((d_n * block, TILE), F32),
            pltpu.VMEM((2, n1, n2), F32),
            pltpu.VMEM((rows * n1, 2 * n2), F32),
            pltpu.VMEM((2 * n1, 2 * n2), F32),
            pltpu.VMEM((2 * n1, 2 * n2), F32),
            pltpu.VMEM((d_n * block, TILE), F32),
            pltpu.VMEM((d_n, c_n, piece, n2), F32),
            pltpu.VMEM((d_n, c_n, piece, n2), F32),
            pltpu.VMEM((c_n, piece, n2), F32),
            pltpu.VMEM((c_n, piece, n2), F32),
            pltpu.VMEM((piece, n2), F32),
            dma((4,)),
            dma((5, d_n)),
            dma((5, d_n)),
            dma((2, c_n)),
            dma((2, c_n)),
        ],
        compiler_params=pltpu.CompilerParams(
            collective_id=0, has_side_effects=True, vmem_limit_bytes=48 * 1024 * 1024),
        name="conv_backward",
    )(
        blocks(out_grad), blocks(saved_input), filters.reshape(groups, chunk, n2),
        jnp.asarray(first), jnp.asarray(last), jnp.asarray(turn_re), jnp.asarray(turn_im),
        jnp.asarray(mid_high), jnp.asarray(mid_low),
    )
    input_grad = input_grad.reshape(d_n, tokens // TILE, rows, TILE).transpose(0, 2, 1, 3)
    input_grad = input_grad.reshape(batch, channels, tokens).astype(BF16)
    return input_grad, filter_grad.reshape(groups, tokens)


def solution(mesh):
    placed = (P(None, "chan", "ctx"), P(None, "chan", "ctx"), P(None, "ctx"))
    return jax.shard_map(
        local,
        mesh=mesh,
        in_specs=placed,
        out_specs=(P(None, "chan", "ctx"), P(None, "ctx")),
        check_vma=False,
    )
```

```python
import functools
import math

import jax
import jax.numpy as jnp
import numpy as np
from jax import lax
from jax.experimental import pallas as pl
from jax.experimental.pallas import tpu as pltpu
from jax.sharding import PartitionSpec as P

LANES = 256
TILE = 128
F32 = jnp.float32
BF16 = jnp.bfloat16


def split_table(table):
    high = table.astype(np.float32).astype(BF16)
    low = (table - high.astype(np.float64)).astype(np.float32).astype(BF16)
    return high, low


def tables(n1, n2):
    length = n1 * n2
    a = np.arange(n1, dtype=np.int64)
    b = np.arange(n2, dtype=np.int64)
    theta = 2.0 * np.pi / (4 * n1) * (np.outer(4 * a + 1, a) % (4 * n1))
    cosine, sine = np.cos(theta), np.sin(theta)
    high, low = split_table(np.concatenate([cosine, -sine], axis=0))
    first = np.concatenate([high, high, low], axis=1)
    high, low = split_table(np.concatenate([cosine.T, sine.T], axis=1) / length)
    last = np.concatenate([high, high, low], axis=1)
    turn = 2.0 * np.pi / (4 * length) * (np.outer(4 * a + 1, b) % (4 * length))
    turn_re = np.cos(turn).astype(np.float32)
    turn_im = (-np.sin(turn)).astype(np.float32)
    phi = 2.0 * np.pi / n2 * (np.outer(b, b) % n2)
    re, im = np.cos(phi), -np.sin(phi)
    mid_high, mid_low = split_table(np.block([[re, im], [-im, re]]))
    return first, last, turn_re, turn_im, mid_high, mid_low


def split(x):
    high = x.astype(BF16)
    return high, (x - high.astype(F32)).astype(BF16)


def dot(a, b):
    return jnp.dot(a, b, preferred_element_type=F32)


def body(
    d_n, c_n, rows, n1, n2, piece,
    og_hbm, sv_hbm, fl_hbm, first_hbm, last_hbm, tr_hbm, ti_hbm, mh_hbm, ml_hbm,
    ig_out, fg_out,
    og_buf, sv_buf, fl_buf, g_spec, h_spec, p_spec, ig_send, fp_send, fp_recv, rs_send, rs_recv, ag_send,
    first_ref, last_ref, tr_ref, ti_ref, mh_ref, ml_ref,
    loc_sem, tab_sem, send_sem, recv_sem, csend_sem, crecv_sem,
):
    me = lax.axis_index("ctx")
    mc = lax.axis_index("chan")
    chunk = n1 // d_n
    halves = n2 // TILE
    block = chunk * halves * rows
    fblock = chunk * halves * 2
    both = 2 if n1 <= 128 else 1
    ahead = [lax.rem(me + o, d_n) for o in range(d_n)]
    behind = [lax.rem(me + d_n - o, d_n) for o in range(d_n)]
    cahead = [lax.rem(mc + o, c_n) for o in range(c_n)]
    cbehind = [lax.rem(mc + c_n - o, c_n) for o in range(c_n)]

    barrier = pltpu.get_barrier_semaphore()
    for o in range(1, d_n):
        pl.semaphore_signal(barrier, inc=1, device_id={"ctx": ahead[o]}, device_id_type=pl.DeviceIdType.MESH)
    for o in range(1, c_n):
        pl.semaphore_signal(barrier, inc=1, device_id={"chan": cahead[o]}, device_id_type=pl.DeviceIdType.MESH)

    def at_rows(ref, index):
        return ref.at[pl.ds(pl.multiple_of(index * block, block), block), :]

    def at_filters(ref, index):
        return ref.at[pl.ds(pl.multiple_of(index * fblock, fblock), fblock), :]

    def at_half(ref, index, half):
        return ref.at[pl.ds(pl.multiple_of(index * block + half * (block // 2), block // 2), block // 2), :]

    def at_piece(ref, index):
        return ref.at[pl.ds(pl.multiple_of(index * piece, piece), piece), :]

    loads = [
        pltpu.make_async_copy(src, dst, tab_sem.at[index])
        for index, (src, dst) in enumerate(
            [(first_hbm, first_ref), (last_hbm, last_ref), (tr_hbm, tr_ref), (ti_hbm, ti_ref), (mh_hbm, mh_ref), (ml_hbm, ml_ref)])
    ]
    locals_ = [
        pltpu.make_async_copy(fl_hbm, at_filters(fl_buf, me), loc_sem.at[0]),
        pltpu.make_async_copy(og_hbm.at[me], at_rows(og_buf, me), loc_sem.at[1]),
        pltpu.make_async_copy(sv_hbm.at[me], at_rows(sv_buf, me), loc_sem.at[2]),
    ]
    for copy in loads + locals_:
        copy.start()
    pl.semaphore_wait(barrier, d_n + c_n - 2)

    def push(kind, o, src, dst):
        return pltpu.make_async_remote_copy(
            src_ref=src, dst_ref=dst, send_sem=send_sem.at[kind, o], recv_sem=recv_sem.at[kind, o],
            device_id={"ctx": ahead[o]}, device_id_type=pl.DeviceIdType.MESH)

    def cpush(kind, o, src, dst):
        return pltpu.make_async_remote_copy(
            src_ref=src, dst_ref=dst, send_sem=csend_sem.at[kind, o], recv_sem=crecv_sem.at[kind, o],
            device_id={"chan": cahead[o]}, device_id_type=pl.DeviceIdType.MESH)

    peers = range(1, d_n)
    sent = []
    for o in peers:
        sent.append(push(0, o, fl_hbm, at_filters(fl_buf, me)))
    for o in peers:
        sent.append(push(1, o, og_hbm.at[ahead[o]], at_rows(og_buf, me)))
    for o in peers:
        sent.append(push(2, o, sv_hbm.at[ahead[o]], at_rows(sv_buf, me)))
    for copy in sent:
        copy.start()

    def first_stage(x):
        high, low = split(x)
        out = dot(first_ref[...], jnp.concatenate([high, low, high], axis=0))
        return turned(out[:n1], out[n1:])

    def turned(re, im):
        tr, ti = tr_ref[...], ti_ref[...]
        return jnp.concatenate([re * tr - im * ti, re * ti + im * tr], axis=1)

    def mid_stage(x):
        high, low = split(x)
        return dot(high, mh_ref[...]) + dot(low, mh_ref[...]) + dot(high, ml_ref[...])

    def last_stage(x):
        x = turned(x[:, :n2], x[:, n2:])
        high, low = split(jnp.concatenate([x[:, :n2], x[:, n2:]], axis=0))
        return dot(last_ref[...], jnp.concatenate([high, low, high], axis=0))

    def stacked(parts):
        return parts[0] if len(parts) == 1 else jnp.concatenate(parts, axis=0)

    def row_of(ref, r, rows=rows):
        parts = [ref[pl.ds(h * rows + r, n1, stride=halves * rows), :] for h in range(halves)]
        return jnp.concatenate(parts, axis=1)

    def spectra(ref, i):
        return mid_stage(stacked([first_stage(row_of(ref, i * both + j)) for j in range(both)]))

    def group_rows(i):
        return pl.ds(pl.multiple_of(lax.rem(i * both, 2) * n1, n1), both * n1)

    def span(i):
        return pl.ds(pl.multiple_of(i * (both * n1), both * n1), both * n1)

    for copy in loads:
        copy.wait()
    locals_[0].wait()
    for o in peers:
        push(0, o, fl_hbm, at_filters(fl_buf, behind[o])).wait_recv()
    for g in range(0, 2, both):
        h_spec[g * n1 : (g + both) * n1, :] = mid_stage(
            stacked([first_stage(row_of(fl_buf, g + j, 2)) for j in range(both)]))

    locals_[1].wait()
    for o in peers:
        push(1, o, og_hbm.at[ahead[o]], at_rows(og_buf, behind[o])).wait_recv()

    def input_step(i, carry):
        grad = spectra(og_buf, i)
        g_spec[span(i), :] = grad
        filt = h_spec[group_rows(i), :]
        gr, gi, hr, hi = grad[:, :n2], grad[:, n2:], filt[:, :n2], filt[:, n2:]
        back = mid_stage(jnp.concatenate([hr * gr + hi * gi, hi * gr - hr * gi], axis=1))
        for j in range(both):
            out = last_stage(back[j * n1 : (j + 1) * n1])
            for h in range(halves):
                ig_send[pl.ds(h * rows + i * both + j, n1, stride=halves * rows), :] = out[:, h * TILE : (h + 1) * TILE]
        return carry

    lax.fori_loop(0, rows // both, input_step, 0)
    own = pltpu.make_async_copy(at_rows(ig_send, me), at_rows(ig_out, me), loc_sem.at[3])
    own.start()
    for o in peers:
        copy = push(3, o, at_half(ig_send, ahead[o], 0), at_half(ig_out, me, 0))
        copy.start()
        sent.append(copy)

    locals_[2].wait()
    for o in peers:
        push(2, o, sv_hbm.at[ahead[o]], at_rows(sv_buf, behind[o])).wait_recv()
    p_spec[...] = jnp.zeros_like(p_spec)

    def filter_step(i, carry):
        spec = spectra(sv_buf, i)
        grad = g_spec[span(i), :]
        xr, xi, gr, gi = spec[:, :n2], spec[:, n2:], grad[:, :n2], grad[:, n2:]
        p_spec[group_rows(i), :] += jnp.concatenate([xr * gr + xi * gi, xi * gr - xr * gi], axis=1)
        return carry

    lax.fori_loop(0, rows // both, filter_step, 0)
    total = mid_stage(p_spec[...])
    for g in range(2):
        part = last_stage(total[g * n1 : (g + 1) * n1])
        for h in range(halves):
            fp_send[pl.ds(h * 2 + g, n1, stride=halves * 2), :] = part[:, h * TILE : (h + 1) * TILE]

    for o in peers:
        copy = push(4, o, at_filters(fp_send, ahead[o]), at_filters(fp_recv, me))
        copy.start()
        sent.append(copy)
    for o in peers:
        copy = push(5, o, at_half(ig_send, ahead[o], 1), at_half(ig_out, me, 1))
        copy.start()
        sent.append(copy)
    for o in peers:
        push(4, o, at_filters(fp_send, ahead[o]), at_filters(fp_recv, behind[o])).wait_recv()
    acc = at_filters(fp_send, me)[...]
    for o in peers:
        acc = acc + at_filters(fp_recv, behind[o])[...]
    rs_send[...] = acc
    for o in range(1, c_n):
        copy = cpush(0, o, at_piece(rs_send, cahead[o]), at_piece(rs_recv, mc))
        copy.start()
        sent.append(copy)
    for o in range(1, c_n):
        cpush(0, o, at_piece(rs_send, cahead[o]), at_piece(rs_recv, cbehind[o])).wait_recv()
    acc = at_piece(rs_send, mc)[...]
    for o in range(1, c_n):
        acc = acc + at_piece(rs_recv, cbehind[o])[...]
    ag_send[...] = acc
    fg_out[pl.ds(pl.multiple_of(mc * piece, piece), piece), :] = acc
    for o in range(1, c_n):
        copy = cpush(1, o, ag_send, at_piece(fg_out, mc))
        copy.start()
        sent.append(copy)
    for o in range(1, c_n):
        cpush(1, o, ag_send, at_piece(fg_out, cbehind[o])).wait_recv()
    for half, kind in ((0, 3), (1, 5)):
        for o in peers:
            push(kind, o, at_half(ig_send, ahead[o], half), at_half(ig_out, behind[o], half)).wait_recv()
    own.wait()
    for copy in sent:
        copy.wait_send()


def local(saved_input, out_grad, filters):
    batch, channels, tokens = saved_input.shape
    groups = filters.shape[0]
    d_n, c_n = lax.axis_size("ctx"), lax.axis_size("chan")
    rows = batch * channels // d_n
    n2 = LANES
    chunk = tokens // n2
    n1 = chunk * d_n
    block = chunk * rows * (n2 // TILE)
    fblock = groups * tokens // TILE
    piece = fblock // c_n
    assert groups == 2 and rows % 2 == 0 and channels % 2 == 0 and piece % 8 == 0
    norm = float(tokens * d_n * batch * (channels // groups) * c_n) ** -0.5

    def blocks(x):
        return x.reshape(d_n, rows, tokens // TILE, TILE).transpose(0, 2, 1, 3).reshape(d_n, block, TILE)

    held = tables(n1, n2)
    any_spec = pl.BlockSpec(memory_space=pl.ANY)
    vmem = pl.BlockSpec(memory_space=pltpu.VMEM)
    dma = pltpu.SemaphoreType.DMA
    input_grad, filter_grad = pl.pallas_call(
        functools.partial(body, d_n, c_n, rows, n1, n2, piece),
        out_shape=[
            jax.ShapeDtypeStruct((d_n * block, TILE), F32),
            jax.ShapeDtypeStruct((fblock, TILE), F32),
        ],
        in_specs=[any_spec] * 9,
        out_specs=[any_spec, vmem],
        scratch_shapes=[
            pltpu.VMEM((d_n * block, TILE), F32),
            pltpu.VMEM((d_n * block, TILE), F32),
            pltpu.VMEM((d_n * fblock, TILE), F32),
            pltpu.VMEM((rows * n1, 2 * n2), F32),
            pltpu.VMEM((2 * n1, 2 * n2), F32),
            pltpu.VMEM((2 * n1, 2 * n2), F32),
            pltpu.VMEM((d_n * block, TILE), F32),
            pltpu.VMEM((d_n * fblock, TILE), F32),
            pltpu.VMEM((d_n * fblock, TILE), F32),
            pltpu.VMEM((fblock, TILE), F32),
            pltpu.VMEM((fblock, TILE), F32),
            pltpu.VMEM((piece, TILE), F32),
        ]
        + [pltpu.VMEM(table.shape, table.dtype) for table in held]
        + [
            dma((4,)),
            dma((len(held),)),
            dma((6, d_n)),
            dma((6, d_n)),
            dma((2, c_n)),
            dma((2, c_n)),
        ],
        compiler_params=pltpu.CompilerParams(
            collective_id=0, has_side_effects=True, vmem_limit_bytes=60 * 1024 * 1024),
        name="conv_backward",
    )(
        blocks(out_grad), blocks(saved_input),
        filters.reshape(groups, tokens // TILE, TILE).transpose(1, 0, 2).reshape(fblock, TILE),
        *(jnp.asarray(table) for table in held),
    )
    input_grad = input_grad.reshape(d_n, tokens // TILE, rows, TILE).transpose(0, 2, 1, 3)
    input_grad = input_grad.reshape(batch, channels, tokens).astype(BF16)
    filter_grad = filter_grad.reshape(tokens // TILE, groups, TILE).transpose(1, 0, 2)
    return input_grad, filter_grad.reshape(groups, tokens) * norm


def solution(mesh):
    placed = (P(None, "chan", "ctx"), P(None, "chan", "ctx"), P(None, "ctx"))
    return jax.shard_map(
        local,
        mesh=mesh,
        in_specs=placed,
        out_specs=(P(None, "chan", "ctx"), P(None, "ctx")),
        check_vma=False,
    )
```

```python
import functools
import math

import jax
import jax.numpy as jnp
import numpy as np
from jax import lax
from jax.experimental import pallas as pl
from jax.experimental.pallas import tpu as pltpu
from jax.sharding import PartitionSpec as P

LANES = 256
TILE = 128
F32 = jnp.float32
BF16 = jnp.bfloat16


def split_table(table):
    high = table.astype(np.float32).astype(BF16)
    low = (table - high.astype(np.float64)).astype(np.float32).astype(BF16)
    return high, low


def tables(n1, n2):
    length = n1 * n2
    a = np.arange(n1, dtype=np.int64)
    b = np.arange(n2, dtype=np.int64)
    theta = 2.0 * np.pi / (4 * n1) * (np.outer(4 * a + 1, a) % (4 * n1))
    cosine, sine = np.cos(theta), np.sin(theta)
    high, low = split_table(np.concatenate([cosine, -sine], axis=0))
    first = np.concatenate([high, high, low], axis=1)
    high, low = split_table(np.concatenate([cosine.T, sine.T], axis=1) / length)
    last = np.concatenate([high, high, low], axis=1)
    turn = 2.0 * np.pi / (4 * length) * (np.outer(4 * a + 1, b) % (4 * length))
    turn_re = np.cos(turn).astype(np.float32)
    turn_im = (-np.sin(turn)).astype(np.float32)
    phi = 2.0 * np.pi / n2 * (np.outer(b, b) % n2)
    re, im = np.cos(phi), -np.sin(phi)
    mid_high, mid_low = split_table(np.block([[re, im], [-im, re]]))
    return first, last, turn_re, turn_im, mid_high, mid_low


def split(x):
    high = x.astype(BF16)
    return high, (x - high.astype(F32)).astype(BF16)


def dot(a, b):
    return jnp.dot(a, b, preferred_element_type=F32)


def body(
    d_n, c_n, rows, n1, n2, piece,
    og_hbm, sv_hbm, fl_hbm, first_hbm, last_hbm, tr_hbm, ti_hbm, mh_hbm, ml_hbm,
    ig_out, fg_out,
    og_buf, sv_buf, fl_buf, g_spec, h_spec, p_spec, ig_send, fp_send, fp_recv, rs_send, rs_recv, ag_send,
    first_ref, last_ref, tr_ref, ti_ref, mh_ref, ml_ref,
    loc_sem, tab_sem, send_sem, recv_sem, csend_sem, crecv_sem, fsend_sem, frecv_sem,
):
    me = lax.axis_index("ctx")
    mc = lax.axis_index("chan")
    chunk = n1 // d_n
    halves = n2 // TILE
    block = chunk * halves * rows
    fblock = chunk * halves * 2
    both = 2 if n1 <= 128 else 1
    ahead = [lax.rem(me + o, d_n) for o in range(d_n)]
    behind = [lax.rem(me + d_n - o, d_n) for o in range(d_n)]
    cahead = [lax.rem(mc + o, c_n) for o in range(c_n)]
    cbehind = [lax.rem(mc + c_n - o, c_n) for o in range(c_n)]

    barrier = pltpu.get_barrier_semaphore()
    for o in range(1, d_n):
        pl.semaphore_signal(barrier, inc=1, device_id={"ctx": ahead[o]}, device_id_type=pl.DeviceIdType.MESH)
    for o in range(1, c_n):
        pl.semaphore_signal(barrier, inc=1, device_id={"chan": cahead[o]}, device_id_type=pl.DeviceIdType.MESH)

    def at_rows(ref, index):
        return ref.at[pl.ds(pl.multiple_of(index * block, block), block), :]

    def at_filters(ref, index):
        return ref.at[pl.ds(pl.multiple_of(index * fblock, fblock), fblock), :]

    def at_half(ref, index, half):
        return ref.at[pl.ds(pl.multiple_of(index * block + half * (block // 2), block // 2), block // 2), :]

    def at_piece(ref, index):
        return ref.at[pl.ds(pl.multiple_of(index * piece, piece), piece), :]

    loads = [
        pltpu.make_async_copy(src, dst, tab_sem.at[index])
        for index, (src, dst) in enumerate(
            [(first_hbm, first_ref), (last_hbm, last_ref), (tr_hbm, tr_ref), (ti_hbm, ti_ref), (mh_hbm, mh_ref), (ml_hbm, ml_ref)])
    ]
    locals_ = [
        pltpu.make_async_copy(fl_hbm, at_filters(fl_buf, me), loc_sem.at[0]),
        pltpu.make_async_copy(og_hbm.at[me], at_rows(og_buf, me), loc_sem.at[1]),
        pltpu.make_async_copy(sv_hbm.at[me], at_rows(sv_buf, me), loc_sem.at[2]),
    ]
    for copy in loads + locals_:
        copy.start()
    pl.semaphore_wait(barrier, d_n + c_n - 2)

    def push(kind, o, src, dst):
        return pltpu.make_async_remote_copy(
            src_ref=src, dst_ref=dst, send_sem=send_sem.at[kind, o], recv_sem=recv_sem.at[kind, o],
            device_id={"ctx": ahead[o]}, device_id_type=pl.DeviceIdType.MESH)

    def cpush(kind, o, src, dst):
        return pltpu.make_async_remote_copy(
            src_ref=src, dst_ref=dst, send_sem=csend_sem.at[kind, o], recv_sem=crecv_sem.at[kind, o],
            device_id={"chan": cahead[o]}, device_id_type=pl.DeviceIdType.MESH)

    def filter_piece(chunk_index, piece_index):
        start = pl.multiple_of(chunk_index * fblock + piece_index * piece, piece)
        return fl_buf.at[pl.ds(start, piece), :]

    def share(o, q, chunk_index, piece_index):
        view = filter_piece(chunk_index, piece_index)
        return pltpu.make_async_remote_copy(
            src_ref=view, dst_ref=view, send_sem=fsend_sem.at[o, q], recv_sem=frecv_sem.at[o, q],
            device_id={"chan": cahead[q]}, device_id_type=pl.DeviceIdType.MESH)

    peers = range(1, d_n)
    sent = []
    for o in peers:
        sent.append(push(0, o, at_piece(fl_hbm, mc), filter_piece(me, mc)))
    for o in peers:
        sent.append(push(1, o, og_hbm.at[ahead[o]], at_rows(og_buf, me)))
    for o in peers:
        sent.append(push(2, o, sv_hbm.at[ahead[o]], at_rows(sv_buf, me)))
    for copy in sent:
        copy.start()

    def first_stage(x):
        high, low = split(x)
        out = dot(first_ref[...], jnp.concatenate([high, low, high], axis=0))
        return turned(out[:n1], out[n1:])

    def turned(re, im):
        tr, ti = tr_ref[...], ti_ref[...]
        return jnp.concatenate([re * tr - im * ti, re * ti + im * tr], axis=1)

    def mid_stage(x):
        high, low = split(x)
        return dot(high, mh_ref[...]) + dot(low, mh_ref[...]) + dot(high, ml_ref[...])

    def last_stage(x):
        x = turned(x[:, :n2], x[:, n2:])
        high, low = split(jnp.concatenate([x[:, :n2], x[:, n2:]], axis=0))
        return dot(last_ref[...], jnp.concatenate([high, low, high], axis=0))

    def stacked(parts):
        return parts[0] if len(parts) == 1 else jnp.concatenate(parts, axis=0)

    def row_of(ref, r, rows=rows):
        parts = [ref[pl.ds(h * rows + r, n1, stride=halves * rows), :] for h in range(halves)]
        return jnp.concatenate(parts, axis=1)

    def spectra(ref, i):
        return mid_stage(stacked([first_stage(row_of(ref, i * both + j)) for j in range(both)]))

    def group_rows(i):
        return pl.ds(pl.multiple_of(lax.rem(i * both, 2) * n1, n1), both * n1)

    def span(i):
        return pl.ds(pl.multiple_of(i * (both * n1), both * n1), both * n1)

    for copy in loads:
        copy.wait()
    locals_[0].wait()
    for o in peers:
        push(0, o, at_piece(fl_hbm, mc), filter_piece(behind[o], mc)).wait_recv()
        for q in range(1, c_n):
            copy = share(o, q, behind[o], mc)
            copy.start()
            sent.append(copy)
    for o in peers:
        for q in range(1, c_n):
            share(o, q, behind[o], cbehind[q]).wait_recv()
    for g in range(0, 2, both):
        h_spec[g * n1 : (g + both) * n1, :] = mid_stage(
            stacked([first_stage(row_of(fl_buf, g + j, 2)) for j in range(both)]))

    locals_[1].wait()
    for o in peers:
        push(1, o, og_hbm.at[ahead[o]], at_rows(og_buf, behind[o])).wait_recv()

    def input_step(i, carry):
        grad = spectra(og_buf, i)
        g_spec[span(i), :] = grad
        filt = h_spec[group_rows(i), :]
        gr, gi, hr, hi = grad[:, :n2], grad[:, n2:], filt[:, :n2], filt[:, n2:]
        back = mid_stage(jnp.concatenate([hr * gr + hi * gi, hi * gr - hr * gi], axis=1))
        for j in range(both):
            out = last_stage(back[j * n1 : (j + 1) * n1])
            for h in range(halves):
                ig_send[pl.ds(h * rows + i * both + j, n1, stride=halves * rows), :] = out[:, h * TILE : (h + 1) * TILE]
        return carry

    lax.fori_loop(0, rows // both, input_step, 0)
    own = pltpu.make_async_copy(at_rows(ig_send, me), at_rows(ig_out, me), loc_sem.at[3])
    own.start()
    for o in peers:
        copy = push(3, o, at_half(ig_send, ahead[o], 0), at_half(ig_out, me, 0))
        copy.start()
        sent.append(copy)

    locals_[2].wait()
    for o in peers:
        push(2, o, sv_hbm.at[ahead[o]], at_rows(sv_buf, behind[o])).wait_recv()
    p_spec[...] = jnp.zeros_like(p_spec)

    def filter_step(i, carry):
        spec = spectra(sv_buf, i)
        grad = g_spec[span(i), :]
        xr, xi, gr, gi = spec[:, :n2], spec[:, n2:], grad[:, :n2], grad[:, n2:]
        p_spec[group_rows(i), :] += jnp.concatenate([xr * gr + xi * gi, xi * gr - xr * gi], axis=1)
        return carry

    lax.fori_loop(0, rows // both, filter_step, 0)
    total = mid_stage(p_spec[...])
    for g in range(2):
        part = last_stage(total[g * n1 : (g + 1) * n1])
        for h in range(halves):
            fp_send[pl.ds(h * 2 + g, n1, stride=halves * 2), :] = part[:, h * TILE : (h + 1) * TILE]

    for o in peers:
        copy = push(4, o, at_filters(fp_send, ahead[o]), at_filters(fp_recv, me))
        copy.start()
        sent.append(copy)
    for o in peers:
        copy = push(5, o, at_half(ig_send, ahead[o], 1), at_half(ig_out, me, 1))
        copy.start()
        sent.append(copy)
    for o in peers:
        push(4, o, at_filters(fp_send, ahead[o]), at_filters(fp_recv, behind[o])).wait_recv()
    acc = at_filters(fp_send, me)[...]
    for o in peers:
        acc = acc + at_filters(fp_recv, behind[o])[...]
    rs_send[...] = acc
    for o in range(1, c_n):
        copy = cpush(0, o, at_piece(rs_send, cahead[o]), at_piece(rs_recv, mc))
        copy.start()
        sent.append(copy)
    for o in range(1, c_n):
        cpush(0, o, at_piece(rs_send, cahead[o]), at_piece(rs_recv, cbehind[o])).wait_recv()
    acc = at_piece(rs_send, mc)[...]
    for o in range(1, c_n):
        acc = acc + at_piece(rs_recv, cbehind[o])[...]
    ag_send[...] = acc
    fg_out[pl.ds(pl.multiple_of(mc * piece, piece), piece), :] = acc
    for o in range(1, c_n):
        copy = cpush(1, o, ag_send, at_piece(fg_out, mc))
        copy.start()
        sent.append(copy)
    for o in range(1, c_n):
        cpush(1, o, ag_send, at_piece(fg_out, cbehind[o])).wait_recv()
    for half, kind in ((0, 3), (1, 5)):
        for o in peers:
            push(kind, o, at_half(ig_send, ahead[o], half), at_half(ig_out, behind[o], half)).wait_recv()
    own.wait()
    for copy in sent:
        copy.wait_send()


def local(saved_input, out_grad, filters):
    batch, channels, tokens = saved_input.shape
    groups = filters.shape[0]
    d_n, c_n = lax.axis_size("ctx"), lax.axis_size("chan")
    rows = batch * channels // d_n
    n2 = LANES
    chunk = tokens // n2
    n1 = chunk * d_n
    block = chunk * rows * (n2 // TILE)
    fblock = groups * tokens // TILE
    piece = fblock // c_n
    assert groups == 2 and rows % 2 == 0 and channels % 2 == 0 and piece % 8 == 0
    norm = float(tokens * d_n * batch * (channels // groups) * c_n) ** -0.5

    def blocks(x):
        return x.reshape(d_n, rows, tokens // TILE, TILE).transpose(0, 2, 1, 3).reshape(d_n, block, TILE)

    held = tables(n1, n2)
    hbm = pl.BlockSpec(memory_space=pltpu.HBM)
    vmem = pl.BlockSpec(memory_space=pltpu.VMEM)
    dma = pltpu.SemaphoreType.DMA
    input_grad, filter_grad = pl.pallas_call(
        functools.partial(body, d_n, c_n, rows, n1, n2, piece),
        out_shape=[
            jax.ShapeDtypeStruct((d_n * block, TILE), F32),
            jax.ShapeDtypeStruct((fblock, TILE), F32),
        ],
        in_specs=[hbm] * 9,
        out_specs=[hbm, vmem],
        scratch_shapes=[
            pltpu.VMEM((d_n * block, TILE), F32),
            pltpu.VMEM((d_n * block, TILE), F32),
            pltpu.VMEM((d_n * fblock, TILE), F32),
            pltpu.VMEM((rows * n1, 2 * n2), F32),
            pltpu.VMEM((2 * n1, 2 * n2), F32),
            pltpu.VMEM((2 * n1, 2 * n2), F32),
            pltpu.VMEM((d_n * block, TILE), F32),
            pltpu.VMEM((d_n * fblock, TILE), F32),
            pltpu.VMEM((d_n * fblock, TILE), F32),
            pltpu.VMEM((fblock, TILE), F32),
            pltpu.VMEM((fblock, TILE), F32),
            pltpu.VMEM((piece, TILE), F32),
        ]
        + [pltpu.VMEM(table.shape, table.dtype) for table in held]
        + [
            dma((4,)),
            dma((len(held),)),
            dma((6, d_n)),
            dma((6, d_n)),
            dma((2, c_n)),
            dma((2, c_n)),
            dma((d_n, c_n)),
            dma((d_n, c_n)),
        ],
        compiler_params=pltpu.CompilerParams(
            collective_id=0, has_side_effects=True, vmem_limit_bytes=60 * 1024 * 1024),
        name="conv_backward",
    )(
        blocks(out_grad), blocks(saved_input),
        filters.reshape(groups, tokens // TILE, TILE).transpose(1, 0, 2).reshape(fblock, TILE),
        *(jnp.asarray(table) for table in held),
    )
    input_grad = input_grad.reshape(d_n, tokens // TILE, rows, TILE).transpose(0, 2, 1, 3)
    input_grad = input_grad.reshape(batch, channels, tokens).astype(BF16)
    filter_grad = filter_grad.reshape(tokens // TILE, groups, TILE).transpose(1, 0, 2)
    return input_grad, filter_grad.reshape(groups, tokens) * norm


def solution(mesh):
    placed = (P(None, "chan", "ctx"), P(None, "chan", "ctx"), P(None, "ctx"))
    return jax.shard_map(
        local,
        mesh=mesh,
        in_specs=placed,
        out_specs=(P(None, "chan", "ctx"), P(None, "ctx")),
        check_vma=False,
    )
```
